128 devices in a mesh: vloop: 8 (over z, y_lo), pairs: 16 (over x, y_hi, core).
Axes of the slice: x: 4, y: 4 (y_hi: 2, y_lo: 2; y = y_hi * 2 + y_lo), z: 4, core: 2. Of those that a mesh axis runs over, the one named last changes fastest.
Arguments:
- factors: float32 [64, 512, 1280], P('vloop', 'pairs'), may hold values from -0.15625 to 0.15625
- amplitudes: float32 [512, 512, 128], P('vloop', 'pairs'), may hold values from -1 to 1
- occ_energy: float32 [96], replicated, may hold values from -2 to -0.5
- virt_energy: float32 [64], replicated, may hold values from 0.2 to 2.5
- pair_list: int32 [128, 2], P('pairs'), may hold values from 0 to 95
Outputs:
- new_amps: float32 [128, 64, 4, 8], P('pairs', 'vloop')
The draws below stay inside these ranges and needn't reach their ends.
Inputs may be any that keep to these rules, and one draw needn't show every extreme that they name: `pair_list`: each entry names an occupied orbital.
All inputs are finite; a program needn't handle non-finite values.
Results may differ from the reference program's by a relative error of at most 0.00016.
Values sent between devices are 32-bit elements; how exact they have to be, the bound alone decides.
No kernel may reach another device: no remote copies, remote signals or barrier semaphores. Data moves between devices by JAX's collectives and lax.ppermute only.
A program may use at most 128 MiB of HBM per device.

```python
import jax
import jax.numpy as jnp
from jax import lax

NO = 96
NV = 512
NAUX = 1280
P_SIZE = 128
ROWS_DEV = 8
STEPS = 4
ROWS = 64


def plant(array, rng, low, high):
    extent = array.shape
    index_at = [jax.random.randint(jax.random.fold_in(rng, axis), (), 0, extent[axis]) for axis in range(len(extent))]
    array = array.at[tuple(index_at)].set(low)
    longest = extent.index(max(extent))
    index_at[longest] = (index_at[longest] + 1) % extent[longest]
    return array.at[tuple(index_at)].set(high)


def block_levels(stream_key, shape, shards, least, high):
    gain, own = 1.0, jax.random.fold_in(stream_key, 6)
    for axis_at, blocks in shards:
        draws = jnp.exp(jax.random.uniform(jax.random.fold_in(own, axis_at), (blocks,), jnp.float32, least / len(shards), high / len(shards)))
        gain = gain * jnp.repeat(draws, shape[axis_at] // blocks).reshape([-1 if axis == axis_at else 1 for axis in range(len(shape))])
    return gain


def centred(key, dims, deviation, most, shards=(), held_as=jnp.bfloat16):
    gain = block_levels(key, dims, shards, -0.22, 0.18) if shards else 1.0
    result = jax.random.normal(key, dims, jnp.float32) * deviation * gain
    return jnp.minimum(jnp.maximum(result, -most), most).astype(held_as)


def setup_inputs(seed: int = 0) -> dict:
    key_list = jax.random.split(jax.random.key(seed), 6)
    return {
        "factors": centred(key_list[0], (ROWS, NV, NAUX), NAUX ** -0.5, 0.15625, ((0, 8), (1, 16)), jnp.float32),
        "amplitudes": centred(key_list[1], (NV, NV, P_SIZE), 0.15, 1.0, ((0, 8), (1, 16)), jnp.float32),
        "occ_energy": jnp.clip(jax.random.uniform(key_list[2], (NO,), jnp.float32, -2.0, -0.5), -2.0, -0.5),
        "virt_energy": jnp.clip(jax.random.uniform(key_list[3], (ROWS,), jnp.float32, 0.2, 2.5), 0.2, 2.5),
        "pair_list": plant(jax.random.randint(key_list[4], (P_SIZE, 2), 0, NO), jax.random.fold_in(key_list[4], 1), 0, NO - 1).astype(jnp.int32),
    }


def reference(factors, amplitudes, occ_energy, virt_energy, pair_list):
    blocks = ROWS // ROWS_DEV
    factor_blocks = factors.reshape(blocks, ROWS_DEV, NV, NAUX)
    occ_pair = occ_energy[pair_list[:, 0]] + occ_energy[pair_list[:, 1]]
    virt_blocks = virt_energy.reshape(blocks, ROWS_DEV)
    step_terms = []
    partner_energy = []
    for step_index in range(STEPS):
        partner = jnp.roll(factor_blocks, step_index, axis=0)

        def per_block(block_index):
            row_side = lax.dynamic_index_in_dim(factor_blocks, block_index, 0, keepdims=False)
            col_side = lax.dynamic_index_in_dim(partner, block_index, 0, keepdims=False)
            integrals = lax.dot_general(row_side.reshape(ROWS_DEV * NV, NAUX), col_side.reshape(ROWS_DEV * NV, NAUX), (((1,), (1,)), ((), ())), precision=lax.Precision.HIGHEST, preferred_element_type=jnp.float32)
            integrals = integrals.reshape(ROWS_DEV, NV, ROWS_DEV, NV)
            return jnp.einsum("acbd,cdp->pab", integrals, amplitudes, precision=lax.Precision.HIGHEST)

        block_terms = lax.map(per_block, jnp.arange(blocks, dtype=jnp.int32))
        step_terms.append(block_terms)
        partner_energy.append(jnp.roll(virt_blocks, step_index, axis=0))
    stacked = jnp.stack(step_terms, axis=0)
    ladder = jnp.transpose(stacked, (2, 1, 3, 0, 4)).reshape(P_SIZE, ROWS, STEPS, ROWS_DEV)
    energy_b = jnp.stack(partner_energy, axis=1)
    energy_b = jnp.broadcast_to(energy_b[:, None, :, :], (blocks, ROWS_DEV, STEPS, ROWS_DEV)).reshape(ROWS, STEPS, ROWS_DEV)
    denominator = virt_energy[None, :, None, None] + energy_b[None] - occ_pair[:, None, None, None]
    return ladder / denominator
```

```python
import jax
import jax.numpy as jnp
from jax import lax
from jax.experimental import pallas as pl
from jax.experimental.pallas import tpu as pltpu
from jax.sharding import Mesh
from jax.sharding import PartitionSpec as P

STEPS = 4
VLOOP = ("z", "yl")
PAIRS = ("x", "yh", "k")
D_CHUNK = 16


def ring(shard, axis, by):
    count = lax.axis_size(axis)
    return lax.ppermute(shard, axis, [(i, (i + by) % count) for i in range(count)])


def y_at(y):
    return (y % 2) * 2 + y // 2


def y_ring(shard, by):
    return lax.ppermute(shard, ("yl", "yh"), [(y_at(y), y_at((y + by) % 4)) for y in range(4)])


def other(shard, axis):
    return lax.ppermute(shard, axis, [(0, 1), (1, 0)])


def split(value):
    high = lax.reduce_precision(value, 8, 7)
    return high.astype(jnp.bfloat16), (value - high).astype(jnp.bfloat16)


def split_in_kernel(value):
    high = value.astype(jnp.bfloat16)
    return high, (value - high.astype(jnp.float32)).astype(jnp.bfloat16)


def dot(lhs, rhs, last):
    return lax.dot_general(
        lhs, rhs, (((1,), (1 if last else 0,)), ((), ())), preferred_element_type=jnp.float32
    )


def ladder_kernel(index_ref, *refs):
    a_refs, refs = refs[:8], refs[8:]
    bh_ref, bl_ref, t_refs, init_ref = refs[0], refs[1], refs[2:6], refs[6]
    out_ref, ah_ref, al_ref, m_ref = refs[7:]
    step = pl.program_id(0)
    aux = bh_ref.shape[-1]
    rows, cols = 8, 32

    @pl.when(step == 0)
    def _():
        out_ref[...] = init_ref[...]
        for part in range(8):
            source, half = divmod(part, 2)
            for row in range(4):
                high, low = split_in_kernel(a_refs[part][row])
                at = (half * 4 + row) * 128 + source * cols
                ah_ref[pl.ds(at, cols), :] = high
                al_ref[pl.ds(at, cols), :] = low

    for s in range(STEPS):
        bh = bh_ref[s].reshape(D_CHUNK * rows, aux)
        bl = bl_ref[s].reshape(D_CHUNK * rows, aux)
        m_ref[s] = dot(bh, ah_ref[...], True) + dot(bh, al_ref[...], True) + dot(bl, ah_ref[...], True)
    total = out_ref[...]
    for pair in range(D_CHUNK // 2):
        weights = jnp.concatenate(
            [t_refs[source][0, 0, 2 * pair + d] for d in range(2) for source in range(4)], axis=0
        )
        lines = []
        for a in range(rows):
            for s in range(STEPS):
                lines.append(
                    jnp.concatenate(
                        [
                            m_ref[s, pl.ds((2 * pair + d) * rows, rows), pl.ds(a * 128, 128)]
                            for d in range(2)
                        ],
                        axis=1,
                    )
                )
        high, low = split_in_kernel(jnp.concatenate(lines, axis=0))
        both = dot(high, weights, False)
        total += both[:, :128] + both[:, 128:] + dot(low, weights[:, :128], False)
    out_ref[...] = total


def ladder_part(index, row, a_parts, b_high, b_low, t_all, init):
    aux = b_high.shape[-1]
    a_specs = [
        pl.BlockSpec((4, 32, aux), lambda i, n, at=at: (at, 0, 0)) for _, at in a_parts
    ]
    b_spec = pl.BlockSpec((STEPS, D_CHUNK, 8, aux), lambda i, n: (0, i, 0, 0))
    t_specs = [
        pl.BlockSpec(
            (1, 1, D_CHUNK, 32, 256), lambda i, n, source=source: (n[source], n[4 + row], i, 0, 0)
        )
        for source in range(4)
    ]
    whole = pl.BlockSpec((256, 128), lambda i, n: (0, 0))
    return pl.pallas_call(
        ladder_kernel,
        grid_spec=pltpu.PrefetchScalarGridSpec(
            num_scalar_prefetch=1,
            grid=(64 // D_CHUNK,),
            in_specs=a_specs + [b_spec, b_spec] + t_specs + [whole],
            out_specs=whole,
            scratch_shapes=[
                pltpu.VMEM((1024, aux), jnp.bfloat16),
                pltpu.VMEM((1024, aux), jnp.bfloat16),
                pltpu.VMEM((STEPS, D_CHUNK * 8, 1024), jnp.float32),
            ],
        ),
        out_shape=jax.ShapeDtypeStruct((256, 128), jnp.float32),
        compiler_params=pltpu.CompilerParams(vmem_limit_bytes=56 * 1024 * 1024),
        name=f"ladder_{row}",
    )(index, *[part for part, _ in a_parts], b_high, b_low, t_all, t_all, t_all, t_all, init)


def local(factors, amplitudes, occ_energy, virt_energy, pair_list):
    z, yl, x, yh, k = (lax.axis_index(name) for name in ("z", "yl", "x", "yh", "k"))
    rows, cols, aux = factors.shape
    own = factors
    halves = (own[:4], own[4:])
    from_lo = ring(own, "x", 1)
    from_hi = ring(own, "x", -1)
    far_lo = ring(from_lo[:4], "x", 1)
    far_hi = ring(from_hi[4:], "x", -1)
    mate_lo = y_ring(y_ring(halves[0], 1), 1)
    mate_hi = y_ring(y_ring(halves[1], -1), -1)
    mates = (mate_lo, mate_hi)
    mate_from_lo = [ring(mate, "x", 1) for mate in mates]
    mate_from_hi = [ring(mate, "x", -1) for mate in mates]
    mate_far_lo = ring(mate_from_lo[0], "x", 1)
    mate_far_hi = ring(mate_from_hi[1], "x", -1)
    turned = jnp.transpose(own, (1, 0, 2))
    below = ring(turned, "z", 1)
    same = lax.ppermute(turned, "yl", [(0, 1)])
    crossed = other(below, "yl")
    deep = lax.ppermute(crossed, ("z", "yl"), [(2 * i, 2 * ((i + 1) % 4)) for i in range(4)])
    odd = yl == 1
    partners = [turned, jnp.where(odd, same, crossed), below, jnp.where(odd, crossed, deep)]
    partners = [jnp.concatenate([part, other(part, "k")], axis=0) for part in partners]
    pieces = [split(part) for part in partners]
    b_high = jnp.stack([high for high, _ in pieces], axis=0)
    b_low = jnp.stack([low for _, low in pieces], axis=0)
    amps = amplitudes.reshape(2, 32, cols, -1)
    keep = jnp.transpose(lax.dynamic_index_in_dim(amps, k, 0, False), (1, 0, 2))
    give = jnp.transpose(lax.dynamic_index_in_dim(amps, 1 - k, 0, False), (1, 0, 2))
    mine = jnp.concatenate([keep, other(give, "k")], axis=0)
    both = [mine, other(mine, "yl")]
    up = [ring(part, "z", -1) for part in both]
    far = [ring(part, "z", -1) for part in up]
    down = [ring(part, "z", 1) for part in both]
    t_all = jnp.stack(
        [
            jnp.stack([jnp.concatenate(split(part), axis=-1) for part in pair], axis=0)
            for pair in (both, up, far, down)
        ],
        axis=0,
    )
    offsets = jnp.array([0, 3, 1, 2], jnp.int32)
    index = jnp.concatenate(
        [jnp.mod(x + offsets - z + 4, 4), jnp.stack([jnp.bitwise_xor(yh, yl), 1 - jnp.bitwise_xor(yh, yl)])]
    ).astype(jnp.int32)
    first = [
        (own, 0), (own, 1), (from_lo, 0), (from_lo, 1), (from_hi, 0), (from_hi, 1), (far_lo, 0), (far_hi, 0)
    ]
    second = [
        (part, 0)
        for part in (*mates, *mate_from_lo, *mate_from_hi, mate_far_lo, mate_far_hi)
    ]
    ladder = jnp.zeros((256, 128), jnp.float32)
    ladder = ladder_part(index, 0, first, b_high, b_low, t_all, ladder)
    ladder = ladder_part(index, 1, second, b_high, b_low, t_all, ladder)
    tiles = jnp.transpose(ladder.reshape(256, 16, 8), (1, 2, 0))
    tiles = lax.all_to_all(tiles, PAIRS, 0, 0, tiled=True)
    summed = jnp.sum(tiles, axis=0).reshape(8, rows, STEPS, rows)
    one_hot = (
        pair_list[:, :, None] == jnp.arange(occ_energy.shape[0], dtype=jnp.int32)[None, None, :]
    ).astype(jnp.float32)
    occ_pair = jnp.sum(one_hot * occ_energy[None, None, :], axis=(1, 2))
    block = z * 2 + yl
    energy_a = lax.dynamic_slice_in_dim(virt_energy, block * rows, rows)
    energy_b = jnp.stack(
        [
            lax.dynamic_slice_in_dim(virt_energy, jnp.mod(block - step + 8, 8) * rows, rows)
            for step in range(STEPS)
        ],
        axis=0,
    )
    denominator = (
        energy_a[None, :, None, None] + energy_b[None, None, :, :] - occ_pair[:, None, None, None]
    )
    return summed / denominator


def solution(mesh):
    torus = Mesh(mesh.devices.reshape(4, 2, 4, 2, 2), ("z", "yl", "x", "yh", "k"))
    in_specs = (P(VLOOP, PAIRS, None), P(VLOOP, PAIRS, None), P(), P(), P(PAIRS, None))
    out_specs = P(PAIRS, VLOOP, None, None)
    return jax.shard_map(local, mesh=torus, in_specs=in_specs, out_specs=out_specs, check_vma=False)
```

```python
import functools

import jax
import jax.numpy as jnp
from jax import lax
from jax.experimental import pallas as pl
from jax.experimental.pallas import tpu as pltpu
from jax.sharding import Mesh
from jax.sharding import PartitionSpec as P


STEPS = 4
held = lax.optimization_barrier
VLOOP = ("z", "yl")
PAIRS = ("x", "yh", "k")


def ring(shard, axis, by):
    count = lax.axis_size(axis)
    return lax.ppermute(shard, axis, [(i, (i + by) % count) for i in range(count)])


def y_at(y):
    return (y % 2) * 2 + y // 2


def y_ring(shard, by):
    return lax.ppermute(shard, ("yl", "yh"), [(y_at(y), y_at((y + by) % 4)) for y in range(4)])


def other(shard, axis):
    return lax.ppermute(shard, axis, [(0, 1), (1, 0)])


def split_in_kernel(value):
    high = value.astype(jnp.bfloat16)
    return high, (value - high.astype(jnp.float32)).astype(jnp.bfloat16)


def dot(lhs, rhs, last):
    return lax.dot_general(
        lhs, rhs, (((1,), (1 if last else 0,)), ((), ())), preferred_element_type=jnp.float32
    )


def ladder_kernel(index_ref, *refs, slots, picked):
    a_refs, refs = refs[:8], refs[8:]
    count = 2 * slots
    b_refs, refs = refs[:count], refs[count:]
    other_refs, refs = (refs[:2], refs[2:]) if picked else ((), refs)
    t_refs, refs = refs[:4], refs[4:]
    out_ref, ah_ref, al_ref, bh_ref, bl_ref, m_ref, acc_ref = refs
    step = pl.program_id(0)
    rows, cols = 8, 32
    depth, aux = b_refs[0].shape[1:]
    block = rows * depth

    @pl.when(step == 0)
    def _():
        acc_ref[...] = jnp.zeros_like(acc_ref)
        for part in range(8):
            source, half = divmod(part, 2)
            for row in range(4):
                high, low = split_in_kernel(a_refs[part][row])
                at = (half * 4 + row) * 128 + source * cols
                ah_ref[pl.ds(at, cols), :] = high
                al_ref[pl.ds(at, cols), :] = low

    for part in range(count):
        value = b_refs[part][...]
        if picked and part >= count - 2:
            value = jnp.where(index_ref[4] == 1, value, other_refs[part - count + 2][...])
        high, low = split_in_kernel(value.reshape(block, aux))
        bh_ref[pl.ds(part * block, block), :] = high
        bl_ref[pl.ds(part * block, block), :] = low
    m = dot(bh_ref[...], ah_ref[...], True)
    m += dot(bh_ref[...], al_ref[...], True)
    m += dot(bl_ref[...], ah_ref[...], True)
    for a in range(rows):
        m_ref[a] = m[:, a * 128 : a * 128 + 128]
    for d in range(depth):
        t_high, t_low = split_in_kernel(
            jnp.concatenate([t_refs[source][0, kk, d] for kk in range(2) for source in range(4)], axis=0)
        )
        lines = [
            jnp.concatenate(
                [m_ref[a, pl.ds((2 * slot + kk) * block + d, rows, stride=depth), :] for kk in range(2)],
                axis=1,
            )
            for slot in range(slots)
            for a in range(rows)
        ]
        high, low = split_in_kernel(jnp.concatenate(lines, axis=0))
        acc_ref[...] += dot(high, jnp.concatenate([t_high, t_low], axis=1), False)
        acc_ref[:, :128] += dot(low, t_high, False)

    @pl.when(step == pl.num_programs(0) - 1)
    def _():
        for slot in range(slots):
            at = pl.ds(slot * 64, 64)
            out_ref[slot] = acc_ref[at, :128] + acc_ref[at, 128:]


def ladder_part(index, a_parts, b_parts, others, t_all):
    aux = b_parts[0].shape[-1]
    slots = len(b_parts) // 2
    depth = 32 // slots
    a_specs = [pl.BlockSpec((4, 32, aux), lambda i, n: (0, 0, 0)) for _ in a_parts]
    b_specs = [pl.BlockSpec((8, depth, aux), lambda i, n: (0, i, 0))] * (len(b_parts) + len(others))
    t_specs = [
        pl.BlockSpec((1, 2, depth, 32, 128), lambda i, n, source=source: (n[source], 0, i, 0, 0))
        for source in range(4)
    ]
    return pl.pallas_call(
        functools.partial(ladder_kernel, slots=slots, picked=bool(others)),
        grid_spec=pltpu.PrefetchScalarGridSpec(
            num_scalar_prefetch=1,
            grid=(32 // depth,),
            in_specs=a_specs + b_specs + t_specs,
            out_specs=pl.BlockSpec((slots, 64, 128), lambda i, n: (0, 0, 0)),
            scratch_shapes=[
                pltpu.VMEM((1024, aux), jnp.bfloat16),
                pltpu.VMEM((1024, aux), jnp.bfloat16),
                pltpu.VMEM((512, aux), jnp.bfloat16),
                pltpu.VMEM((512, aux), jnp.bfloat16),
                pltpu.VMEM((8, 512, 128), jnp.float32),
                pltpu.VMEM((slots * 64, 256), jnp.float32),
            ],
        ),
        out_shape=jax.ShapeDtypeStruct((slots, 64, 128), jnp.float32),
        compiler_params=pltpu.CompilerParams(vmem_limit_bytes=60 * 1024 * 1024),
    )(index, *a_parts, *b_parts, *others, *([t_all] * 4))


def along_x(lo, hi):
    from_lo = [ring(half, "x", 1) for half in (lo, hi)]
    from_hi = [ring(half, "x", -1) for half in (lo, hi)]
    far = [ring(from_lo[0], "x", 1), ring(from_hi[1], "x", -1)]
    return [lo, hi, *from_lo, *from_hi, *far]


def ladder_over_denominator(factors, amplitudes, occ_energy, virt_energy, pair_list):
    z, yl, x, yh, k = (lax.axis_index(name) for name in ("z", "yl", "x", "yh", "k"))
    rows, cols, _ = factors.shape
    own = factors
    odd, low_y, edge = yl == 1, yh == 0, yl == yh
    halves = (held(own[:4]), held(own[4:]))
    guest, passing, home = [], [], []
    for half in halves:
        above, under = y_ring(half, -1), y_ring(half, 1)
        kept, passed = held((jnp.where(low_y, above, under), jnp.where(low_y, under, above)))
        guest.append(kept)
        passing.append(passed)
    for half, passed in zip(halves, passing):
        hop = lax.ppermute(passed, ("yl", "yh"), [(y_at(0), y_at(1)), (y_at(3), y_at(2))])
        home.append(held(jnp.where(edge, half, hop)))
    guest_rows = along_x(*guest)
    home_rows = along_x(*home)
    sibling = held(jnp.concatenate([jnp.where(edge, g, p) for g, p in zip(guest, passing)], axis=0))
    below = ring(own, "z", 1)
    crossed = ring(sibling, "z", 1)
    onward = [(i, (i + 2) % 8) for i in range(8)]
    deep_a = lax.ppermute(below, ("z", "yl"), onward[1::2])
    deep_b = lax.ppermute(crossed, ("z", "yl"), onward[0::2])
    own, sibling, below, crossed, deep_a, deep_b = (
        (part, other(part, "k"))
        for part in (
            own, sibling, below,
            crossed, deep_a, deep_b,
        )
    )
    amps = amplitudes.reshape(2, 32, cols, -1)
    keep = jnp.transpose(lax.dynamic_index_in_dim(amps, k, 0, False), (1, 0, 2))
    give = jnp.transpose(lax.dynamic_index_in_dim(amps, 1 - k, 0, False), (1, 0, 2))
    mine = held(jnp.stack([keep, other(give, "k")], axis=0))
    up = ring(mine, "z", -1)
    far = ring(up, "z", -1)
    down = ring(far, "z", -1)
    t_all = jnp.zeros((4, *mine.shape), jnp.float32)
    for at, part in ((0, mine), (1, up), (2, far), (3, down)):
        t_all = held(t_all.at[at].set(part))
    sources = jnp.mod(x + jnp.array([0, 3, 1, 2], jnp.int32) - z + 4, 4)
    index = jnp.concatenate([sources, jnp.reshape(yl, (1,))]).astype(jnp.int32)
    guest_part = jnp.concatenate(
        [
            ladder_part(index, guest_rows, (*sibling, *below), (), t_all),
            ladder_part(index, guest_rows, (*crossed, *deep_a), own, t_all),
        ],
        axis=0,
    )
    home_part = ladder_part(index, home_rows, (*own, *below, *crossed, *sibling), deep_b, t_all)
    ours, theirs = home_part, other(guest_part, "yl")
    ladder = jnp.stack(
        [
            ours[0] + theirs[0],
            jnp.where(odd, ours[3] + theirs[3], ours[2] + theirs[1]),
            ours[1] + theirs[2],
            jnp.where(odd, ours[2] + theirs[1], ours[3] + theirs[3]),
        ],
        axis=0,
    )
    tiles = jnp.transpose(ladder.reshape(256, 16, 8), (1, 2, 0))
    tiles = lax.all_to_all(tiles, PAIRS, 0, 0, tiled=True)
    summed = jnp.transpose(jnp.sum(tiles, axis=0).reshape(8, STEPS, rows, rows), (0, 2, 1, 3))
    one_hot = (
        pair_list[:, :, None] == jnp.arange(occ_energy.shape[0], dtype=jnp.int32)[None, None, :]
    ).astype(jnp.float32)
    occ_pair = jnp.sum(one_hot * occ_energy[None, None, :], axis=(1, 2))
    block = z * 2 + yl
    energy_a = lax.dynamic_slice_in_dim(virt_energy, block * rows, rows)
    energy_b = jnp.stack(
        [
            lax.dynamic_slice_in_dim(virt_energy, jnp.mod(block - step + 8, 8) * rows, rows)
            for step in range(STEPS)
        ],
        axis=0,
    )
    denominator = (
        energy_a[None, :, None, None] + energy_b[None, None, :, :] - occ_pair[:, None, None, None]
    )
    return summed / denominator


def solution(mesh):
    torus = Mesh(mesh.devices.reshape(4, 2, 4, 2, 2), ("z", "yl", "x", "yh", "k"))
    in_specs = (P(VLOOP, PAIRS, None), P(VLOOP, PAIRS, None), P(), P(), P(PAIRS, None))
    out_specs = P(PAIRS, VLOOP, None, None)
    return jax.shard_map(ladder_over_denominator, mesh=torus, in_specs=in_specs, out_specs=out_specs, check_vma=False)
```

```python
import functools

import jax
import jax.numpy as jnp
from jax import lax
from jax.experimental import pallas as pl
from jax.experimental.pallas import tpu as pltpu
from jax.sharding import Mesh
from jax.sharding import PartitionSpec as P


STEPS = 4
held = lax.optimization_barrier
VLOOP = ("z", "yl")
PAIRS = ("x", "yh", "k")


def ring(shard, axis, by):
    count = lax.axis_size(axis)
    return lax.ppermute(shard, axis, [(i, (i + by) % count) for i in range(count)])


def y_at(y):
    return (y % 2) * 2 + y // 2


def y_ring(shard, by):
    return lax.ppermute(shard, ("yl", "yh"), [(y_at(y), y_at((y + by) % 4)) for y in range(4)])


def other(shard, axis):
    return lax.ppermute(shard, axis, [(0, 1), (1, 0)])


def split_in_kernel(value):
    high = value.astype(jnp.bfloat16)
    return high, (value - high.astype(jnp.float32)).astype(jnp.bfloat16)


def dot(lhs, rhs, last):
    return lax.dot_general(
        lhs, rhs, (((1,), (1 if last else 0,)), ((), ())), preferred_element_type=jnp.float32
    )


def ladder_kernel(index_ref, *refs, slots, picked):
    a_refs, refs = refs[:8], refs[8:]
    count = 2 * slots
    b_refs, refs = refs[:count], refs[count:]
    other_refs, refs = (refs[:2], refs[2:]) if picked else ((), refs)
    t_refs, refs = refs[:4], refs[4:]
    out_ref, ah_ref, al_ref, bh_ref, bl_ref, t_ref, m_ref, acc_ref = refs
    step = pl.program_id(0)
    rows, cols = 8, 32
    depth, aux = b_refs[0].shape[1:]
    block = rows * depth

    @pl.when(step == 0)
    def _():
        acc_ref[...] = jnp.zeros_like(acc_ref)
        for part in range(8):
            source, half = divmod(part, 2)
            for row in range(4):
                high, low = split_in_kernel(a_refs[part][row])
                at = (half * 4 + row) * 128 + source * cols
                ah_ref[pl.ds(at, cols), :] = high
                al_ref[pl.ds(at, cols), :] = low

    for part in range(count):
        value = b_refs[part][...]
        if picked and part >= count - 2:
            value = jnp.where(index_ref[4] == 1, value, other_refs[part - count + 2][...])
        high, low = split_in_kernel(value.reshape(block, aux))
        bh_ref[pl.ds(part * block, block), :] = high
        bl_ref[pl.ds(part * block, block), :] = low
    for near in range(4):
        high, low = split_in_kernel(t_refs[near][...])
        for kk in range(2):
            at = pl.ds(pl.multiple_of(kk * 128 + index_ref[near] * cols, cols), cols)
            t_ref[:, at, :128] = high[kk]
            t_ref[:, at, 128:] = low[kk]
    m = dot(bh_ref[...], ah_ref[...], True)
    m += dot(bh_ref[...], al_ref[...], True)
    m += dot(bl_ref[...], ah_ref[...], True)
    for a in range(rows):
        m_ref[a] = m[:, a * 128 : a * 128 + 128]
    for d in range(depth):
        lines = [
            jnp.concatenate(
                [m_ref[a, pl.ds((2 * slot + kk) * block + d, rows, stride=depth), :] for kk in range(2)],
                axis=1,
            )
            for slot in range(slots)
            for a in range(rows)
        ]
        high, low = split_in_kernel(jnp.concatenate(lines, axis=0))
        acc_ref[...] += dot(high, t_ref[d], False)
        acc_ref[:, :128] += dot(low, t_ref[d, :, :128], False)

    @pl.when(step == pl.num_programs(0) - 1)
    def _():
        for slot in range(slots):
            at = pl.ds(slot * 64, 64)
            out_ref[slot] = acc_ref[at, :128] + acc_ref[at, 128:]


def ladder_part(index, a_parts, b_parts, others, t_parts):
    aux = b_parts[0].shape[-1]
    slots = len(b_parts) // 2
    depth = 32 // slots
    a_specs = [pl.BlockSpec((4, 32, aux), lambda i, n: (0, 0, 0)) for _ in a_parts]
    b_specs = [pl.BlockSpec((8, depth, aux), lambda i, n: (0, i, 0))] * (len(b_parts) + len(others))
    t_specs = [pl.BlockSpec((2, depth, 32, 128), lambda i, n: (0, i, 0, 0))] * 4
    return pl.pallas_call(
        functools.partial(ladder_kernel, slots=slots, picked=bool(others)),
        grid_spec=pltpu.PrefetchScalarGridSpec(
            num_scalar_prefetch=1,
            grid=(32 // depth,),
            in_specs=a_specs + b_specs + t_specs,
            out_specs=pl.BlockSpec((slots, 64, 128), lambda i, n: (0, 0, 0)),
            scratch_shapes=[
                pltpu.VMEM((1024, aux), jnp.bfloat16),
                pltpu.VMEM((1024, aux), jnp.bfloat16),
                pltpu.VMEM((512, aux), jnp.bfloat16),
                pltpu.VMEM((512, aux), jnp.bfloat16),
                pltpu.VMEM((depth, 256, 256), jnp.bfloat16),
                pltpu.VMEM((8, 512, 128), jnp.float32),
                pltpu.VMEM((slots * 64, 256), jnp.float32),
            ],
        ),
        out_shape=jax.ShapeDtypeStruct((slots, 64, 128), jnp.float32),
        compiler_params=pltpu.CompilerParams(vmem_limit_bytes=60 * 1024 * 1024),
    )(index, *a_parts, *b_parts, *others, *t_parts)


def along_x(lo, hi):
    from_lo = [ring(half, "x", 1) for half in (lo, hi)]
    from_hi = [ring(half, "x", -1) for half in (lo, hi)]
    far = [ring(from_lo[0], "x", 1), ring(from_hi[1], "x", -1)]
    return [lo, hi, *from_lo, *from_hi, *far]


def ladder_over_denominator(factors, amplitudes, occ_energy, virt_energy, pair_list):
    z, yl, x, yh, k = (lax.axis_index(name) for name in ("z", "yl", "x", "yh", "k"))
    rows, cols, _ = factors.shape
    own = factors
    odd, low_y, edge = yl == 1, yh == 0, yl == yh
    halves = (held(own[:4]), held(own[4:]))
    guest, passing, home = [], [], []
    for half in halves:
        above, under = y_ring(half, -1), y_ring(half, 1)
        kept, passed = held((jnp.where(low_y, above, under), jnp.where(low_y, under, above)))
        guest.append(kept)
        passing.append(passed)
    for half, passed in zip(halves, passing):
        hop = lax.ppermute(passed, ("yl", "yh"), [(y_at(0), y_at(1)), (y_at(3), y_at(2))])
        home.append(held(jnp.where(edge, half, hop)))
    guest_rows = along_x(*guest)
    home_rows = along_x(*home)
    sibling = held(jnp.concatenate([jnp.where(edge, g, p) for g, p in zip(guest, passing)], axis=0))
    below = ring(own, "z", 1)
    onward = [(i, (i + 2) % 8) for i in range(8)]
    crossed_y = lax.ppermute(below, ("yl", "yh"), [(y_at(1), y_at(0)), (y_at(3), y_at(2))])
    crossed_z = lax.ppermute(sibling, ("z", "yl"), onward[1::2])
    deep_a = lax.ppermute(below, ("z", "yl"), onward[1::2])
    deep_b = lax.ppermute(crossed_y, ("z", "yl"), onward[0::2])
    crossed = held(jnp.where(odd, crossed_z, crossed_y))
    own, sibling, below, crossed, deep_a, deep_b = (
        (part, other(part, "k"))
        for part in (
            own, sibling, below,
            crossed, deep_a, deep_b,
        )
    )
    amps = amplitudes.reshape(2, 32, cols, -1)
    keep = jnp.transpose(lax.dynamic_index_in_dim(amps, k, 0, False), (1, 0, 2))
    give = jnp.transpose(lax.dynamic_index_in_dim(amps, 1 - k, 0, False), (1, 0, 2))
    mine = held(jnp.stack([keep, other(give, "k")], axis=0))
    up = ring(mine, "z", -1)
    far = ring(up, "z", -1)
    down = ring(far, "z", -1)
    t_parts = (mine, up, far, down)
    away = jnp.mod(z - x + jnp.arange(4, dtype=jnp.int32) + 4, 4)
    places = jnp.where(away == 0, 0, jnp.where(away == 3, 1, jnp.where(away == 1, 2, 3)))
    index = jnp.concatenate([places, jnp.reshape(yl, (1,))]).astype(jnp.int32)
    guest_a = ladder_part(index, guest_rows, (*sibling, *below), (), t_parts)
    guest_b = ladder_part(index, guest_rows, (*crossed, *deep_a), own, t_parts)
    home_part = ladder_part(index, home_rows, (*own, *below, *crossed, *sibling), deep_b, t_parts)
    ours, theirs = home_part, (*other(guest_a, "yl"), *other(guest_b, "yl"))
    ladder = jnp.stack(
        [
            ours[0] + theirs[0],
            jnp.where(odd, ours[3] + theirs[3], ours[2] + theirs[1]),
            ours[1] + theirs[2],
            jnp.where(odd, ours[2] + theirs[1], ours[3] + theirs[3]),
        ],
        axis=0,
    )
    tiles = jnp.transpose(ladder.reshape(256, 16, 8), (1, 2, 0))
    tiles = lax.all_to_all(tiles, PAIRS, 0, 0, tiled=True)
    summed = jnp.transpose(jnp.sum(tiles, axis=0).reshape(8, STEPS, rows, rows), (0, 2, 1, 3))
    one_hot = (
        pair_list[:, :, None] == jnp.arange(occ_energy.shape[0], dtype=jnp.int32)[None, None, :]
    ).astype(jnp.float32)
    occ_pair = jnp.sum(one_hot * occ_energy[None, None, :], axis=(1, 2))
    block = z * 2 + yl
    energy_a = lax.dynamic_slice_in_dim(virt_energy, block * rows, rows)
    energy_b = jnp.stack(
        [
            lax.dynamic_slice_in_dim(virt_energy, jnp.mod(block - step + 8, 8) * rows, rows)
            for step in range(STEPS)
        ],
        axis=0,
    )
    denominator = (
        energy_a[None, :, None, None] + energy_b[None, None, :, :] - occ_pair[:, None, None, None]
    )
    return summed / denominator


def solution(mesh):
    torus = Mesh(mesh.devices.reshape(4, 2, 4, 2, 2), ("z", "yl", "x", "yh", "k"))
    in_specs = (P(VLOOP, PAIRS, None), P(VLOOP, PAIRS, None), P(), P(), P(PAIRS, None))
    out_specs = P(PAIRS, VLOOP, None, None)
    return jax.shard_map(ladder_over_denominator, mesh=torus, in_specs=in_specs, out_specs=out_specs, check_vma=False)
```

```python
import functools

import jax
import jax.numpy as jnp
from jax import lax
from jax.experimental import pallas as pl
from jax.experimental.pallas import tpu as pltpu
from jax.sharding import Mesh
from jax.sharding import PartitionSpec as P


STEPS = 4
held = lax.optimization_barrier
VLOOP = ("z", "yl")
PAIRS = ("x", "yh", "k")


def ring(shard, axis, by):
    count = lax.axis_size(axis)
    return lax.ppermute(shard, axis, [(i, (i + by) % count) for i in range(count)])


def y_at(y):
    return (y % 2) * 2 + y // 2


def y_ring(shard, by):
    return lax.ppermute(shard, ("yl", "yh"), [(y_at(y), y_at((y + by) % 4)) for y in range(4)])


def other(shard, axis):
    return lax.ppermute(shard, axis, [(0, 1), (1, 0)])


def split_in_kernel(value):
    high = value.astype(jnp.bfloat16)
    return high, (value - high.astype(jnp.float32)).astype(jnp.bfloat16)


def dot(lhs, rhs, last):
    return lax.dot_general(
        lhs, rhs, (((1,), (1 if last else 0,)), ((), ())), preferred_element_type=jnp.float32
    )


def ladder_kernel(index_ref, *refs, slots, picked):
    a_refs, refs = refs[:8], refs[8:]
    count = 2 * slots
    b_refs, refs = refs[:count], refs[count:]
    other_refs, refs = (refs[:2], refs[2:]) if picked else ((), refs)
    t_refs, refs = refs[:4], refs[4:]
    out_ref, ah_ref, al_ref, bh_ref, bl_ref, t_ref, m_ref, acc_ref = refs
    step = pl.program_id(0)
    rows, cols = 8, 32
    depth, aux = b_refs[0].shape[1:]
    block = rows * depth

    @pl.when(step == 0)
    def _():
        acc_ref[...] = jnp.zeros_like(acc_ref)
        for part in range(8):
            source, half = divmod(part, 2)
            for row in range(4):
                high, low = split_in_kernel(a_refs[part][row])
                at = (half * 4 + row) * 128 + source * cols
                ah_ref[pl.ds(at, cols), :] = high
                al_ref[pl.ds(at, cols), :] = low

    for part in range(count):
        value = b_refs[part][...]
        if picked and part >= count - 2:
            value = jnp.where(index_ref[4] == 1, value, other_refs[part - count + 2][...])
        high, low = split_in_kernel(value.reshape(block, aux))
        bh_ref[pl.ds(part * block, block), :] = high
        bl_ref[pl.ds(part * block, block), :] = low
    for near in range(4):
        high, low = split_in_kernel(t_refs[near][...])
        for kk in range(2):
            at = pl.ds(pl.multiple_of(kk * 128 + index_ref[near] * cols, cols), cols)
            t_ref[:, at, :128] = high[kk]
            t_ref[:, at, 128:] = low[kk]
    m = dot(bh_ref[...], ah_ref[...], True)
    m += dot(bh_ref[...], al_ref[...], True)
    m += dot(bl_ref[...], ah_ref[...], True)
    for a in range(rows):
        m_ref[a] = m[:, a * 128 : a * 128 + 128]
    for d in range(depth):
        lines = [
            jnp.concatenate(
                [m_ref[a, pl.ds((2 * slot + kk) * block + d, rows, stride=depth), :] for kk in range(2)],
                axis=1,
            )
            for slot in range(slots)
            for a in range(rows)
        ]
        high, low = split_in_kernel(jnp.concatenate(lines, axis=0))
        acc_ref[...] += dot(high, t_ref[d], False)
        acc_ref[:, :128] += dot(low, t_ref[d, :, :128], False)

    @pl.when(step == pl.num_programs(0) - 1)
    def _():
        for slot in range(slots):
            at = pl.ds(slot * 64, 64)
            out_ref[slot] = acc_ref[at, :128] + acc_ref[at, 128:]


def ladder_part(index, a_parts, b_parts, others, t_parts):
    aux = b_parts[0].shape[-1]
    slots = len(b_parts) // 2
    depth = 32 // slots
    a_specs = [pl.BlockSpec((4, 32, aux), lambda i, n: (0, 0, 0)) for _ in a_parts]
    b_specs = [pl.BlockSpec((8, depth, aux), lambda i, n: (0, i, 0))] * (len(b_parts) + len(others))
    t_specs = [pl.BlockSpec((2, depth, 32, 128), lambda i, n: (0, i, 0, 0))] * 4
    return pl.pallas_call(
        functools.partial(ladder_kernel, slots=slots, picked=bool(others)),
        grid_spec=pltpu.PrefetchScalarGridSpec(
            num_scalar_prefetch=1,
            grid=(32 // depth,),
            in_specs=a_specs + b_specs + t_specs,
            out_specs=pl.BlockSpec((slots, 64, 128), lambda i, n: (0, 0, 0)),
            scratch_shapes=[
                pltpu.VMEM((1024, aux), jnp.bfloat16),
                pltpu.VMEM((1024, aux), jnp.bfloat16),
                pltpu.VMEM((512, aux), jnp.bfloat16),
                pltpu.VMEM((512, aux), jnp.bfloat16),
                pltpu.VMEM((depth, 256, 256), jnp.bfloat16),
                pltpu.VMEM((8, 512, 128), jnp.float32),
                pltpu.VMEM((slots * 64, 256), jnp.float32),
            ],
        ),
        out_shape=jax.ShapeDtypeStruct((slots, 64, 128), jnp.float32),
        compiler_params=pltpu.CompilerParams(vmem_limit_bytes=60 * 1024 * 1024),
    )(index, *a_parts, *b_parts, *others, *t_parts)


def along_x(lo, hi):
    from_lo = [ring(half, "x", 1) for half in (lo, hi)]
    from_hi = [ring(half, "x", -1) for half in (lo, hi)]
    far = [ring(from_lo[0], "x", 1), ring(from_hi[1], "x", -1)]
    return [lo, hi, *from_lo, *from_hi, *far]


def ladder_over_denominator(factors, amplitudes, occ_energy, virt_energy, pair_list):
    z, yl, x, yh, k = (lax.axis_index(name) for name in ("z", "yl", "x", "yh", "k"))
    rows, cols, _ = factors.shape
    own = factors
    odd, low_y, edge = yl == 1, yh == 0, yl == yh
    halves = (held(own[:4]), held(own[4:]))
    guest, passing, home = [], [], []
    for half in halves:
        above, under = y_ring(half, -1), y_ring(half, 1)
        kept, passed = held((jnp.where(low_y, above, under), jnp.where(low_y, under, above)))
        guest.append(kept)
        passing.append(passed)
    for half, passed in zip(halves, passing):
        hop = lax.ppermute(passed, ("yl", "yh"), [(y_at(0), y_at(1)), (y_at(3), y_at(2))])
        home.append(held(jnp.where(edge, half, hop)))
    guest_rows = along_x(*guest)
    home_rows = along_x(*home)
    sibling = held(jnp.concatenate([jnp.where(edge, g, p) for g, p in zip(guest, passing)], axis=0))
    below = ring(own, "z", 1)
    onward = [(i, (i + 2) % 8) for i in range(8)]
    inner = [(i * 4 + y_at(y), (i * 4 + 4) % 16 + y_at(y)) for i in range(4) for y in (1, 2)]
    crossed_y = lax.ppermute(below, ("yl", "yh"), [(y_at(1), y_at(0)), (y_at(2), y_at(3))])
    crossed_z = lax.ppermute(sibling, ("z", "yl", "yh"), inner)
    crossed = held(jnp.where(edge, crossed_y, crossed_z))
    deep_a = lax.ppermute(below, ("z", "yl"), onward[1::2])
    deep_b = lax.ppermute(crossed, ("z", "yl"), onward[0::2])
    own, sibling, below, crossed, deep_a, deep_b = (
        (part, other(part, "k"))
        for part in (
            own, sibling, below,
            crossed, deep_a, deep_b,
        )
    )
    amps = amplitudes.reshape(2, 32, cols, -1)
    keep = jnp.transpose(lax.dynamic_index_in_dim(amps, k, 0, False), (1, 0, 2))
    give = jnp.transpose(lax.dynamic_index_in_dim(amps, 1 - k, 0, False), (1, 0, 2))
    mine = held(jnp.stack([keep, other(give, "k")], axis=0))
    up = ring(mine, "z", -1)
    far = ring(up, "z", -1)
    down = ring(far, "z", -1)
    t_parts = (mine, up, far, down)
    away = jnp.mod(z - x + jnp.arange(4, dtype=jnp.int32) + 4, 4)
    places = jnp.where(away == 0, 0, jnp.where(away == 3, 1, jnp.where(away == 1, 2, 3)))
    index = jnp.concatenate([places, jnp.reshape(yl, (1,))]).astype(jnp.int32)
    guest_cols = (*sibling, *below, *crossed, *deep_a)
    guest_part = ladder_part(index, guest_rows, guest_cols, own, t_parts)
    home_part = ladder_part(index, home_rows, (*own, *below, *crossed, *sibling), deep_b, t_parts)
    ours, theirs = home_part, other(guest_part, "yl")
    ladder = jnp.stack(
        [
            ours[0] + theirs[0],
            jnp.where(odd, ours[3] + theirs[3], ours[2] + theirs[1]),
            ours[1] + theirs[2],
            jnp.where(odd, ours[2] + theirs[1], ours[3] + theirs[3]),
        ],
        axis=0,
    )
    tiles = jnp.transpose(ladder.reshape(256, 16, 8), (1, 2, 0))
    tiles = lax.all_to_all(tiles, PAIRS, 0, 0, tiled=True)
    summed = jnp.transpose(jnp.sum(tiles, axis=0).reshape(8, STEPS, rows, rows), (0, 2, 1, 3))
    one_hot = (
        pair_list[:, :, None] == jnp.arange(occ_energy.shape[0], dtype=jnp.int32)[None, None, :]
    ).astype(jnp.float32)
    occ_pair = jnp.sum(one_hot * occ_energy[None, None, :], axis=(1, 2))
    block = z * 2 + yl
    energy_a = lax.dynamic_slice_in_dim(virt_energy, block * rows, rows)
    energy_b = jnp.stack(
        [
            lax.dynamic_slice_in_dim(virt_energy, jnp.mod(block - step + 8, 8) * rows, rows)
            for step in range(STEPS)
        ],
        axis=0,
    )
    denominator = (
        energy_a[None, :, None, None] + energy_b[None, None, :, :] - occ_pair[:, None, None, None]
    )
    return summed / denominator


def solution(mesh):
    torus = Mesh(mesh.devices.reshape(4, 2, 4, 2, 2), ("z", "yl", "x", "yh", "k"))
    in_specs = (P(VLOOP, PAIRS, None), P(VLOOP, PAIRS, None), P(), P(), P(PAIRS, None))
    out_specs = P(PAIRS, VLOOP, None, None)
    return jax.shard_map(ladder_over_denominator, mesh=torus, in_specs=in_specs, out_specs=out_specs, check_vma=False)
```

```python
import functools

import jax
import jax.numpy as jnp
from jax import lax
from jax.experimental import pallas as pl
from jax.experimental.pallas import tpu as pltpu
from jax.sharding import Mesh
from jax.sharding import PartitionSpec as P


STEPS = 4
held = lax.optimization_barrier
VLOOP = ("z", "yl")
PAIRS = ("x", "yh", "k")


def ring(shard, axis, by):
    count = lax.axis_size(axis)
    return lax.ppermute(shard, axis, [(i, (i + by) % count) for i in range(count)])


def y_at(y):
    return (y % 2) * 2 + y // 2


def y_ring(shard, by):
    return lax.ppermute(shard, ("yl", "yh"), [(y_at(y), y_at((y + by) % 4)) for y in range(4)])


def other(shard, axis):
    return lax.ppermute(shard, axis, [(0, 1), (1, 0)])


def split_in_kernel(value):
    high = value.astype(jnp.bfloat16)
    return high, (value - high.astype(jnp.float32)).astype(jnp.bfloat16)


def dot(lhs, rhs, last):
    return lax.dot_general(
        lhs, rhs, (((1,), (1 if last else 0,)), ((), ())), preferred_element_type=jnp.float32
    )


def ladder_kernel(index_ref, *refs, slots, picked):
    a_refs, refs = refs[:8], refs[8:]
    count = 2 * slots
    b_refs, refs = refs[:count], refs[count:]
    other_refs, refs = (refs[:2], refs[2:]) if picked else ((), refs)
    t_refs, refs = refs[:4], refs[4:]
    out_ref, ah_ref, al_ref, bh_ref, bl_ref, t_ref, m_ref, acc_ref = refs
    step = pl.program_id(0)
    rows, cols = 8, 32
    depth, aux = b_refs[0].shape[1:]
    block = rows * depth

    @pl.when(step == 0)
    def _():
        acc_ref[...] = jnp.zeros_like(acc_ref)
        for part in range(8):
            source, half = divmod(part, 2)
            for row in range(4):
                high, low = split_in_kernel(a_refs[part][row])
                at = (half * 4 + row) * 128 + source * cols
                ah_ref[pl.ds(at, cols), :] = high
                al_ref[pl.ds(at, cols), :] = low

    for part in range(count):
        value = b_refs[part][...]
        if picked and part >= count - 2:
            value = jnp.where(index_ref[4] == 1, value, other_refs[part - count + 2][...])
        high, low = split_in_kernel(value.reshape(block, aux))
        bh_ref[pl.ds(part * block, block), :] = high
        bl_ref[pl.ds(part * block, block), :] = low
    for near in range(4):
        high, low = split_in_kernel(t_refs[near][...])
        for kk in range(2):
            at = pl.ds(pl.multiple_of(kk * 128 + index_ref[near] * cols, cols), cols)
            t_ref[:, at, :128] = high[kk]
            t_ref[:, at, 128:] = low[kk]
    m = dot(bh_ref[...], ah_ref[...], True)
    m += dot(bh_ref[...], al_ref[...], True)
    m += dot(bl_ref[...], ah_ref[...], True)
    for a in range(rows):
        m_ref[a] = m[:, a * 128 : a * 128 + 128]
    for d in range(depth):
        lines = [
            jnp.concatenate(
                [m_ref[a, pl.ds((2 * slot + kk) * block + d, rows, stride=depth), :] for kk in range(2)],
                axis=1,
            )
            for slot in range(slots)
            for a in range(rows)
        ]
        high, low = split_in_kernel(jnp.concatenate(lines, axis=0))
        acc_ref[...] += dot(high, t_ref[d], False)
        acc_ref[:, :128] += dot(low, t_ref[d, :, :128], False)

    @pl.when(step == pl.num_programs(0) - 1)
    def _():
        for slot in range(slots):
            at = pl.ds(slot * 64, 64)
            out_ref[slot] = acc_ref[at, :128] + acc_ref[at, 128:]


def ladder_part(index, a_parts, b_parts, others, t_parts):
    aux = b_parts[0].shape[-1]
    slots = len(b_parts) // 2
    depth = 32 // slots
    a_specs = [pl.BlockSpec((4, 32, aux), lambda i, n: (0, 0, 0)) for _ in a_parts]
    b_specs = [pl.BlockSpec((8, depth, aux), lambda i, n: (0, i, 0))] * (len(b_parts) + len(others))
    t_specs = [pl.BlockSpec((2, depth, 32, 128), lambda i, n: (0, i, 0, 0))] * 4
    return pl.pallas_call(
        functools.partial(ladder_kernel, slots=slots, picked=bool(others)),
        grid_spec=pltpu.PrefetchScalarGridSpec(
            num_scalar_prefetch=1,
            grid=(32 // depth,),
            in_specs=a_specs + b_specs + t_specs,
            out_specs=pl.BlockSpec((slots, 64, 128), lambda i, n: (0, 0, 0)),
            scratch_shapes=[
                pltpu.VMEM((1024, aux), jnp.bfloat16),
                pltpu.VMEM((1024, aux), jnp.bfloat16),
                pltpu.VMEM((512, aux), jnp.bfloat16),
                pltpu.VMEM((512, aux), jnp.bfloat16),
                pltpu.VMEM((depth, 256, 256), jnp.bfloat16),
                pltpu.VMEM((8, 512, 128), jnp.float32),
                pltpu.VMEM((slots * 64, 256), jnp.float32),
            ],
        ),
        out_shape=jax.ShapeDtypeStruct((slots, 64, 128), jnp.float32),
        compiler_params=pltpu.CompilerParams(vmem_limit_bytes=60 * 1024 * 1024),
    )(index, *a_parts, *b_parts, *others, *t_parts)


def along_x(lo, hi):
    from_lo = [ring(half, "x", 1) for half in (lo, hi)]
    from_hi = [ring(half, "x", -1) for half in (lo, hi)]
    far = [ring(from_lo[0], "x", 1), ring(from_hi[1], "x", -1)]
    return [lo, hi, *from_lo, *from_hi, *far]


def ladder_over_denominator(factors, amplitudes, occ_energy, virt_energy, pair_list):
    z, yl, x, yh, k = (lax.axis_index(name) for name in ("z", "yl", "x", "yh", "k"))
    rows, cols, _ = factors.shape
    own = factors
    odd, low_y, edge = yl == 1, yh == 0, yl == yh
    halves = (held(own[:4]), held(own[4:]))
    guest, passing, home = [], [], []
    for half in halves:
        above, under = y_ring(half, -1), y_ring(half, 1)
        kept, passed = held((jnp.where(low_y, above, under), jnp.where(low_y, under, above)))
        guest.append(kept)
        passing.append(passed)
    for half, passed in zip(halves, passing):
        hop = lax.ppermute(passed, ("yl", "yh"), [(y_at(0), y_at(1)), (y_at(3), y_at(2))])
        home.append(held(jnp.where(edge, half, hop)))
    guest_rows = along_x(*guest)
    home_rows = along_x(*home)
    sibling = [held(jnp.where(edge, g, p)) for g, p in zip(guest, passing)]
    below = ring(own, "z", 1)
    onward = [(i, (i + 2) % 8) for i in range(8)]
    inner = [(i * 4 + y_at(y), (i * 4 + 4) % 16 + y_at(y)) for i in range(4) for y in (1, 2)]
    crossed_y = lax.ppermute(below, ("yl", "yh"), [(y_at(1), y_at(0)), (y_at(2), y_at(3))])
    crossed_z = [lax.ppermute(sibling[i], ("z", "yl", "yh"), inner) for i in range(2)]
    crossed = held(jnp.where(edge, crossed_y, jnp.concatenate(crossed_z, axis=0)))
    sibling = held(jnp.concatenate(sibling, axis=0))
    deep_a = lax.ppermute(below, ("z", "yl"), onward[1::2])
    deep_b = lax.ppermute(crossed, ("z", "yl"), onward[0::2])
    own, sibling, below, crossed, deep_a, deep_b = (
        (part, other(part, "k"))
        for part in (
            own, sibling, below,
            crossed, deep_a, deep_b,
        )
    )
    amps = amplitudes.reshape(2, 32, cols, -1)
    keep = jnp.transpose(lax.dynamic_index_in_dim(amps, k, 0, False), (1, 0, 2))
    give = jnp.transpose(lax.dynamic_index_in_dim(amps, 1 - k, 0, False), (1, 0, 2))
    mine = held(jnp.stack([keep, other(give, "k")], axis=0))
    up = ring(mine, "z", -1)
    far = ring(up, "z", -1)
    down = ring(far, "z", -1)
    t_parts = (mine, up, far, down)
    away = jnp.mod(z - x + jnp.arange(4, dtype=jnp.int32) + 4, 4)
    places = jnp.where(away == 0, 0, jnp.where(away == 3, 1, jnp.where(away == 1, 2, 3)))
    index = jnp.concatenate([places, jnp.reshape(yl, (1,))]).astype(jnp.int32)
    guest_cols = (*sibling, *below, *crossed, *deep_a)
    guest_part = ladder_part(index, guest_rows, guest_cols, own, t_parts)
    home_part = ladder_part(index, home_rows, (*own, *below, *crossed, *sibling), deep_b, t_parts)
    ours, theirs = home_part, other(guest_part, "yl")
    ladder = jnp.stack(
        [
            ours[0] + theirs[0],
            jnp.where(odd, ours[3] + theirs[3], ours[2] + theirs[1]),
            ours[1] + theirs[2],
            jnp.where(odd, ours[2] + theirs[1], ours[3] + theirs[3]),
        ],
        axis=0,
    )
    tiles = jnp.transpose(ladder.reshape(256, 16, 8), (1, 2, 0))
    tiles = lax.all_to_all(tiles, PAIRS, 0, 0, tiled=True)
    summed = jnp.transpose(jnp.sum(tiles, axis=0).reshape(8, STEPS, rows, rows), (0, 2, 1, 3))
    one_hot = (
        pair_list[:, :, None] == jnp.arange(occ_energy.shape[0], dtype=jnp.int32)[None, None, :]
    ).astype(jnp.float32)
    occ_pair = jnp.sum(one_hot * occ_energy[None, None, :], axis=(1, 2))
    block = z * 2 + yl
    energy_a = lax.dynamic_slice_in_dim(virt_energy, block * rows, rows)
    energy_b = jnp.stack(
        [
            lax.dynamic_slice_in_dim(virt_energy, jnp.mod(block - step + 8, 8) * rows, rows)
            for step in range(STEPS)
        ],
        axis=0,
    )
    denominator = (
        energy_a[None, :, None, None] + energy_b[None, None, :, :] - occ_pair[:, None, None, None]
    )
    return summed / denominator


def solution(mesh):
    torus = Mesh(mesh.devices.reshape(4, 2, 4, 2, 2), ("z", "yl", "x", "yh", "k"))
    in_specs = (P(VLOOP, PAIRS, None), P(VLOOP, PAIRS, None), P(), P(), P(PAIRS, None))
    out_specs = P(PAIRS, VLOOP, None, None)
    return jax.shard_map(ladder_over_denominator, mesh=torus, in_specs=in_specs, out_specs=out_specs, check_vma=False)
```

```python
import functools

import jax
import jax.numpy as jnp
from jax import lax
from jax.experimental import pallas as pl
from jax.experimental.pallas import tpu as pltpu
from jax.sharding import Mesh
from jax.sharding import PartitionSpec as P


STEPS = 4
held = lax.optimization_barrier
VLOOP = ("z", "yl")
PAIRS = ("x", "yh", "k")


def ring(shard, axis, by):
    count = lax.axis_size(axis)
    return lax.ppermute(shard, axis, [(i, (i + by) % count) for i in range(count)])


def y_at(y):
    return (y % 2) * 2 + y // 2


def y_ring(shard, by):
    return lax.ppermute(shard, ("yl", "yh"), [(y_at(y), y_at((y + by) % 4)) for y in range(4)])


def other(shard, axis):
    return lax.ppermute(shard, axis, [(0, 1), (1, 0)])


def split_in_kernel(value):
    high = value.astype(jnp.bfloat16)
    return high, (value - high.astype(jnp.float32)).astype(jnp.bfloat16)


def dot(lhs, rhs, last):
    return lax.dot_general(
        lhs, rhs, (((1,), (1 if last else 0,)), ((), ())), preferred_element_type=jnp.float32
    )


def ladder_kernel(index_ref, *refs, slots, picked):
    a_refs, refs = refs[:8], refs[8:]
    count = 2 * slots
    b_refs, refs = refs[:count], refs[count:]
    other_refs, refs = (refs[:2], refs[2:]) if picked else ((), refs)
    t_refs, refs = refs[:4], refs[4:]
    out_ref, ah_ref, al_ref, bh_ref, bl_ref, t_ref, m_ref, acc_ref = refs
    step = pl.program_id(0)
    rows, cols = 8, 32
    depth, aux = b_refs[0].shape[1:]
    block = rows * depth

    @pl.when(step == 0)
    def _():
        acc_ref[...] = jnp.zeros_like(acc_ref)
        for part in range(8):
            source, half = divmod(part, 2)
            for row in range(4):
                high, low = split_in_kernel(a_refs[part][row])
                at = (half * 4 + row) * 128 + source * cols
                ah_ref[pl.ds(at, cols), :] = high
                al_ref[pl.ds(at, cols), :] = low

    for part in range(count):
        value = b_refs[part][...]
        if picked and part >= count - 2:
            value = jnp.where(index_ref[4] == 1, value, other_refs[part - count + 2][...])
        high, low = split_in_kernel(value.reshape(block, aux))
        bh_ref[pl.ds(part * block, block), :] = high
        bl_ref[pl.ds(part * block, block), :] = low
    for near in range(4):
        high, low = split_in_kernel(t_refs[near][...])
        for kk in range(2):
            at = pl.ds(pl.multiple_of(kk * 128 + index_ref[near] * cols, cols), cols)
            t_ref[:, at, :128] = high[kk]
            t_ref[:, at, 128:] = low[kk]
    m = dot(bh_ref[...], ah_ref[...], True)
    m += dot(bh_ref[...], al_ref[...], True)
    m += dot(bl_ref[...], ah_ref[...], True)
    for a in range(rows):
        m_ref[a] = m[:, a * 128 : a * 128 + 128]
    for d in range(depth):
        lines = [
            jnp.concatenate(
                [m_ref[a, pl.ds((2 * slot + kk) * block + d, rows, stride=depth), :] for kk in range(2)],
                axis=1,
            )
            for slot in range(slots)
            for a in range(rows)
        ]
        high, low = split_in_kernel(jnp.concatenate(lines, axis=0))
        acc_ref[...] += dot(high, t_ref[d], False)
        acc_ref[:, :128] += dot(low, t_ref[d, :, :128], False)

    @pl.when(step == pl.num_programs(0) - 1)
    def _():
        for slot in range(slots):
            at = pl.ds(slot * 64, 64)
            out_ref[slot] = acc_ref[at, :128] + acc_ref[at, 128:]


def ladder_part(index, a_parts, b_parts, others, t_parts):
    aux = b_parts[0].shape[-1]
    slots = len(b_parts) // 2
    depth = 32 // slots
    a_specs = [pl.BlockSpec((4, 32, aux), lambda i, n: (0, 0, 0)) for _ in a_parts]
    b_specs = [pl.BlockSpec((8, depth, aux), lambda i, n: (0, i, 0))] * (len(b_parts) + len(others))
    t_specs = [pl.BlockSpec((2, depth, 32, 128), lambda i, n: (0, i, 0, 0))] * 4
    return pl.pallas_call(
        functools.partial(ladder_kernel, slots=slots, picked=bool(others)),
        grid_spec=pltpu.PrefetchScalarGridSpec(
            num_scalar_prefetch=1,
            grid=(32 // depth,),
            in_specs=a_specs + b_specs + t_specs,
            out_specs=pl.BlockSpec((slots, 64, 128), lambda i, n: (0, 0, 0)),
            scratch_shapes=[
                pltpu.VMEM((1024, aux), jnp.bfloat16),
                pltpu.VMEM((1024, aux), jnp.bfloat16),
                pltpu.VMEM((512, aux), jnp.bfloat16),
                pltpu.VMEM((512, aux), jnp.bfloat16),
                pltpu.VMEM((depth, 256, 256), jnp.bfloat16),
                pltpu.VMEM((8, 512, 128), jnp.float32),
                pltpu.VMEM((slots * 64, 256), jnp.float32),
            ],
        ),
        out_shape=jax.ShapeDtypeStruct((slots, 64, 128), jnp.float32),
        compiler_params=pltpu.CompilerParams(vmem_limit_bytes=60 * 1024 * 1024),
    )(index, *a_parts, *b_parts, *others, *t_parts)


def along_x(lo, hi):
    from_lo = [ring(half, "x", 1) for half in (lo, hi)]
    from_hi = [ring(half, "x", -1) for half in (lo, hi)]
    far = [ring(from_lo[0], "x", 1), ring(from_hi[1], "x", -1)]
    return [lo, hi, *from_lo, *from_hi, *far]


def ladder_over_denominator(factors, amplitudes, occ_energy, virt_energy, pair_list):
    z, yl, x, yh, k = (lax.axis_index(name) for name in ("z", "yl", "x", "yh", "k"))
    rows, cols, _ = factors.shape
    own = factors
    odd, low_y, edge = yl == 1, yh == 0, yl == yh
    halves = (held(own[:4]), held(own[4:]))
    guest, passing, home = [], [], []
    for half in halves:
        above, under = y_ring(half, -1), y_ring(half, 1)
        kept, passed = held((jnp.where(low_y, above, under), jnp.where(low_y, under, above)))
        guest.append(kept)
        passing.append(passed)
    for half, passed in zip(halves, passing):
        hop = lax.ppermute(passed, ("yl", "yh"), [(y_at(0), y_at(1)), (y_at(3), y_at(2))])
        home.append(held(jnp.where(edge, half, hop)))
    guest_rows = along_x(*guest)
    home_rows = along_x(*home)
    sibling = [held(jnp.where(edge, g, p)) for g, p in zip(guest, passing)]
    below = ring(own, "z", 1)
    onward = [(i, (i + 2) % 8) for i in range(8)]
    inner = [(i * 4 + y_at(y), (i * 4 + 4) % 16 + y_at(y)) for i in range(4) for y in (1, 2)]
    crossed_y = lax.ppermute(below, ("yl", "yh"), [(y_at(1), y_at(0)), (y_at(2), y_at(3))])
    crossed_z = [lax.ppermute(sibling[i], ("z", "yl", "yh"), inner) for i in range(2)]
    crossed = held(jnp.where(edge, crossed_y, jnp.concatenate(crossed_z, axis=0)))
    sibling = held(jnp.concatenate(sibling, axis=0))
    deep_a = lax.ppermute(below, ("z", "yl"), onward[1::2])
    deep_b = lax.ppermute(crossed, ("z", "yl"), onward[0::2])
    own, sibling, below, crossed, deep_a, deep_b = (
        (part, other(part, "k"))
        for part in (
            own, sibling, below,
            crossed, deep_a, deep_b,
        )
    )
    amps = amplitudes.reshape(2, 32, cols, -1)
    keep = jnp.transpose(lax.dynamic_index_in_dim(amps, k, 0, False), (1, 0, 2))
    give = jnp.transpose(lax.dynamic_index_in_dim(amps, 1 - k, 0, False), (1, 0, 2))
    mine = held(jnp.stack([keep, other(give, "k")], axis=0))
    up = ring(mine, "z", -1)
    far = ring(up, "z", -1)
    down = ring(far, "z", -1)
    t_parts = (mine, up, far, down)
    away = jnp.mod(z - x + jnp.arange(4, dtype=jnp.int32) + 4, 4)
    places = jnp.where(away == 0, 0, jnp.where(away == 3, 1, jnp.where(away == 1, 2, 3)))
    index = jnp.concatenate([places, jnp.reshape(yl, (1,))]).astype(jnp.int32)
    guest_a = ladder_part(index, guest_rows, (*sibling, *below), (), t_parts)
    guest_b = ladder_part(index, guest_rows, (*crossed, *deep_a), own, t_parts)
    home_part = ladder_part(index, home_rows, (*own, *below, *crossed, *sibling), deep_b, t_parts)
    ours, theirs = home_part, (*other(guest_a, "yl"), *other(guest_b, "yl"))
    ladder = jnp.stack(
        [
            ours[0] + theirs[0],
            jnp.where(odd, ours[3] + theirs[3], ours[2] + theirs[1]),
            ours[1] + theirs[2],
            jnp.where(odd, ours[2] + theirs[1], ours[3] + theirs[3]),
        ],
        axis=0,
    )
    tiles = jnp.transpose(ladder.reshape(256, 16, 8), (1, 2, 0))
    tiles = lax.all_to_all(tiles, PAIRS, 0, 0, tiled=True)
    summed = jnp.transpose(jnp.sum(tiles, axis=0).reshape(8, STEPS, rows, rows), (0, 2, 1, 3))
    one_hot = (
        pair_list[:, :, None] == jnp.arange(occ_energy.shape[0], dtype=jnp.int32)[None, None, :]
    ).astype(jnp.float32)
    occ_pair = jnp.sum(one_hot * occ_energy[None, None, :], axis=(1, 2))
    block = z * 2 + yl
    energy_a = lax.dynamic_slice_in_dim(virt_energy, block * rows, rows)
    energy_b = jnp.stack(
        [
            lax.dynamic_slice_in_dim(virt_energy, jnp.mod(block - step + 8, 8) * rows, rows)
            for step in range(STEPS)
        ],
        axis=0,
    )
    denominator = (
        energy_a[None, :, None, None] + energy_b[None, None, :, :] - occ_pair[:, None, None, None]
    )
    return summed / denominator


def solution(mesh):
    torus = Mesh(mesh.devices.reshape(4, 2, 4, 2, 2), ("z", "yl", "x", "yh", "k"))
    in_specs = (P(VLOOP, PAIRS, None), P(VLOOP, PAIRS, None), P(), P(), P(PAIRS, None))
    out_specs = P(PAIRS, VLOOP, None, None)
    return jax.shard_map(ladder_over_denominator, mesh=torus, in_specs=in_specs, out_specs=out_specs, check_vma=False)
```
